32 devices in a mesh: member: 8 (over z, y), region: 4 (over x, core).
Axes of the slice: x: 2, y: 2, z: 4, core: 2. Of those that a mesh axis runs over, the one named last changes fastest.
Arguments:
- background_realizations: float32 [1024, 32768], P('member', 'region'), may hold values from -6 to 6
- realization_expected_data: float32 [1024, 16384], P('member', 'region'), may hold values from -6 to 6
- departure_values: float32 [1024, 16384], P('member', 'region'), may hold values from -6 to 6
- instrument_dispersion: float32 [16384], P('region'), may hold values from 0.5 to 2
- window_piece_offsets: int32 [4, 9], P('region'), may hold values from 0 to 64, as said below
- window_data_pieces: int32 [4, 8, 4], P('region'), may hold values from 0 to 39, as said below
- neighbor_piece_ids: int32 [4, 2, 4], P('region'), may hold values from 0 to 31, as said below
- coupling_indicator: int32 [4, 64, 4], P('region'), may hold values 0 or 1
Outputs:
- analysis: float32 [1024, 32768], P('member', 'region')
The draws below stay inside these ranges and needn't reach their ends.
Inputs may be any that keep to these rules, and one draw needn't show every extreme that they name: `window_piece_offsets`: each row starts at 0, ends at 64 and rises by 1 or more at each entry; entry p lies within 3 of p * 8; in every row one patch spans exactly 14 blocks. `window_data_pieces`: entries index a region's extended observation blocks: 0 to 31 its own, then 4 received from the region before it, then 4 from the region after it; the 4 entries of a patch differ. `neighbor_piece_ids`: entries index the sending region's own observation blocks; the 4 entries of a row differ.
All inputs are finite; a program needn't handle non-finite values. No bound on the sum of `coupling_indicator` on one device may be relied on, other than what follows from the above.
Results may differ from the reference program's by a relative error of at most 0.0003.
Values sent between devices are 32-bit elements; how exact they have to be, the bound alone decides.
A program may use at most 128 MiB of HBM per device.

```python
import math
import jax
import jax.numpy as jnp
from jax import lax

REALIZATION_NUM = 1024
PIECE_LENGTH = 128
OBS_PER = 4
LOCAL = 512
BLK_DEV = 8
HALF = 3
SEGMENTS_AREA = 64
OBSERVED_PARTS = 32
HB = 4
EXT = 40
DOMAIN_NUMBER = 4
PATCHES = 8
N_REGION = 4


def distinct_rows(key, shape_lead, choices, keep):
    scores = jax.random.randint(key, shape_lead + (choices,), 0, 2 ** 20) * choices
    scores = scores + jnp.arange(choices).astype(jnp.int32)
    order = jnp.argsort(scores, axis=-1, stable=True)
    return order[..., :keep].astype(jnp.int32)


def draw_window_piece_offsets(key, part):
    first_key, second_key = jax.random.split(jax.random.fold_in(key, 11))
    offsets = jax.random.randint(first_key, (DOMAIN_NUMBER, PATCHES + 1), -HALF, HALF + 1)
    chosen_patch = jax.random.randint(second_key, (DOMAIN_NUMBER, 1), 1, PATCHES - 1)
    column = jnp.arange(PATCHES + 1)[None, :]
    offsets = jnp.where(column == chosen_patch, -HALF, offsets)
    offsets = jnp.where(column == chosen_patch + 1, HALF, offsets)
    offsets = jnp.where((column == 0) | (column == PATCHES), 0, offsets)
    return (column * BLK_DEV + offsets).astype(jnp.int32)


def draw_window_data_pieces(key, part):
    return distinct_rows(jax.random.fold_in(key, 23), (DOMAIN_NUMBER, PATCHES), EXT, OBS_PER)


def draw_neighbor_piece_ids(key, part):
    return distinct_rows(jax.random.fold_in(key, 37), (DOMAIN_NUMBER, 2), OBSERVED_PARTS, HB)


def with_ends(drawn, key, least, top_value):
    longest = drawn.shape.index(max(drawn.shape))
    spots = []
    for shift in (0, 1):
        where = [jax.random.randint(jax.random.fold_in(key, axis), (), 0, length) for axis, length in enumerate(drawn.shape)]
        where[longest] = (where[longest] + shift) % drawn.shape[longest]
        spots.append(tuple(where))
    return drawn.at[spots[0]].set(least).at[spots[1]].set(top_value)


def levels(own_key, shape, cuts, low, top_value):
    loudness = 1.0
    for dim, blocks in cuts:
        steps = jax.random.uniform(jax.random.fold_in(jax.random.fold_in(own_key, 6), dim), (blocks,), jnp.float32, low / len(cuts), top_value / len(cuts))
        loudness = loudness * jnp.repeat(jnp.exp(steps), shape[dim] // blocks).reshape((-1,) + (1,) * (len(shape) - 1 - dim))
    return loudness


def gaussian(key, dims, width, most, cuts=(), kind=jnp.bfloat16):
    values = jax.random.normal(key, dims, jnp.float32) * width
    if len(cuts) > 0:
        values = levels(key, dims, cuts, -0.22, 0.18) * values
    return jnp.clip(values, min=-most, max=most).astype(kind)


def setup_inputs(seed: int = 0) -> dict:
    arg_keys = jax.random.split(jax.random.key(seed), 9)
    background_realizations = gaussian(arg_keys[0], (REALIZATION_NUM, DOMAIN_NUMBER * SEGMENTS_AREA * PIECE_LENGTH), 1.0, 6.0, ((0, 8), (1, 4)), jnp.float32)
    realization_expected_data = gaussian(arg_keys[1], (REALIZATION_NUM, DOMAIN_NUMBER * OBSERVED_PARTS * PIECE_LENGTH), 1.0, 6.0, ((0, 8), (1, 4)), jnp.float32)
    departure_values = gaussian(arg_keys[2], (REALIZATION_NUM, DOMAIN_NUMBER * OBSERVED_PARTS * PIECE_LENGTH), 1.0, 6.0, ((0, 8), (1, 4)), jnp.float32)
    instrument_dispersion = jnp.clip(jnp.exp(math.log(2.0) - 1.3862944 * jax.random.uniform(arg_keys[3], (DOMAIN_NUMBER * OBSERVED_PARTS * PIECE_LENGTH,), jnp.float32) ** levels(arg_keys[3], (DOMAIN_NUMBER * OBSERVED_PARTS * PIECE_LENGTH,), ((0, 4),), -0.2, 0.2)), 0.5, 2.0)
    window_piece_offsets = draw_window_piece_offsets(jax.random.fold_in(arg_keys[8], 71), 0)
    window_data_pieces = draw_window_data_pieces(jax.random.fold_in(arg_keys[8], 71), 0)
    neighbor_piece_ids = draw_neighbor_piece_ids(jax.random.fold_in(arg_keys[8], 71), 0)
    coupling_indicator = with_ends((jax.random.randint(arg_keys[7], (DOMAIN_NUMBER, SEGMENTS_AREA, OBS_PER), 0, 4) < 3).astype(jnp.int32), jax.random.fold_in(arg_keys[7], 1), 0, 1)
    return dict(background_realizations=background_realizations, realization_expected_data=realization_expected_data, departure_values=departure_values, instrument_dispersion=instrument_dispersion, window_piece_offsets=window_piece_offsets, window_data_pieces=window_data_pieces, neighbor_piece_ids=neighbor_piece_ids, coupling_indicator=coupling_indicator)


highest = lax.Precision.HIGHEST

def listed(stack, lists, axis_at):
    return jax.vmap(lambda region_data, region_list: jnp.take(region_data, region_list, axis=axis_at))(stack, lists)

def extended(stack, neighbor_piece_ids, axis_at):
    before = jnp.roll(listed(stack, neighbor_piece_ids[:, 0], axis_at), 1, axis=0)
    after = jnp.roll(listed(stack, neighbor_piece_ids[:, 1], axis_at), -1, axis=0)
    return jnp.concatenate([stack, before, after], axis=axis_at + 1)

def reference(background_realizations, realization_expected_data, departure_values, instrument_dispersion, window_piece_offsets, window_data_pieces, neighbor_piece_ids, coupling_indicator):
    realization_records = REALIZATION_NUM
    domain_records = N_REGION
    sample_vectors = background_realizations.reshape(realization_records, domain_records, SEGMENTS_AREA, PIECE_LENGTH).transpose(1, 0, 2, 3)
    expected_data = realization_expected_data.reshape(realization_records, domain_records, OBSERVED_PARTS, PIECE_LENGTH).transpose(1, 0, 2, 3)
    innovated = departure_values.reshape(realization_records, domain_records, OBSERVED_PARTS, PIECE_LENGTH).transpose(1, 0, 2, 3)
    variance = instrument_dispersion.reshape(domain_records, OBSERVED_PARTS, PIECE_LENGTH)
    pred_ext = extended(expected_data, neighbor_piece_ids, 1)
    innov_ext = extended(innovated, neighbor_piece_ids, 1)
    var_ext = extended(variance, neighbor_piece_ids, 0)

    def one_region(inputs):
        states, pred_region, innov_region, var_region, bounds_row, lists_row, cover_rows = inputs
        centred = states - jnp.mean(states, axis=0, keepdims=True)

        def solve_patch(chosen):
            raw = jnp.take(pred_region, chosen, axis=1).reshape(realization_records, LOCAL)
            perturbed = raw - jnp.mean(raw, axis=0, keepdims=True)
            local_innov = jnp.take(innov_region, chosen, axis=1).reshape(realization_records, LOCAL)
            local_var = jnp.take(var_region, chosen, axis=0).reshape(LOCAL)
            cov_obs = jnp.dot(perturbed.T.astype(jnp.float32), perturbed.astype(jnp.float32), precision=highest, preferred_element_type=jnp.float32) / (realization_records - 1.0)
            cov_obs = cov_obs + jnp.diag(local_var)
            factor = jnp.linalg.cholesky(cov_obs)
            weights = jax.scipy.linalg.cho_solve((factor, True), local_innov.T)
            return (perturbed, weights)
        perts, weights_all = lax.map(solve_patch, lists_row)
        block_ids = jnp.arange(SEGMENTS_AREA).astype(jnp.int32)
        owners = jnp.sum((bounds_row[None, 1:-1] <= block_ids[:, None]).astype(jnp.int32), axis=1)

        def one_block(block_inputs):
            column, owner_id, mark_row = block_inputs
            perturbed = perts[owner_id]
            weights = weights_all[owner_id]
            kalman_gain = jnp.dot(column.T.astype(jnp.float32), perturbed.astype(jnp.float32), precision=highest, preferred_element_type=jnp.float32) / (realization_records - 1.0)
            kalman_gain = kalman_gain * jnp.repeat(mark_row.astype(jnp.float32), PIECE_LENGTH)[None, :]
            return jnp.dot(weights.T.astype(jnp.float32), kalman_gain.T.astype(jnp.float32), precision=highest, preferred_element_type=jnp.float32)
        increments = lax.map(one_block, (centred.transpose(1, 0, 2), owners, cover_rows))
        return states + increments.transpose(1, 0, 2)
    analysed = lax.map(one_region, (sample_vectors, pred_ext, innov_ext, var_ext, window_piece_offsets, window_data_pieces, coupling_indicator))
    return analysed.transpose(1, 0, 2, 3).reshape(realization_records, domain_records * SEGMENTS_AREA * PIECE_LENGTH)
```

```python
import functools

import jax
import jax.numpy as jnp
from jax import lax
from jax.experimental import pallas as pl
from jax.experimental.pallas import tpu as pltpu
from jax.sharding import PartitionSpec as P

PIECE_LENGTH = 128
OBS_PER = 4
LOCAL = 512


highest = lax.Precision.HIGHEST
high = lax.Precision.HIGH


def shifted(block, axis, distance):
    count = lax.axis_size(axis)
    return lax.ppermute(block, axis, [(i, (i + distance) % count) for i in range(count)])


def pieces(start, count=1):
    return pl.ds(pl.multiple_of(start * PIECE_LENGTH, PIECE_LENGTH), count * PIECE_LENGTH)


def halo_kernel(ids_ref, expected_ref, innov_ref, after_ref, before_ref):
    count = ids_ref.shape[1]
    for side, out_ref in ((0, after_ref), (1, before_ref)):
        for k in range(count):
            source = pieces(ids_ref[side, k])
            out_ref[:, k * PIECE_LENGTH : (k + 1) * PIECE_LENGTH] = expected_ref[:, source]
            out_ref[:, (count + k) * PIECE_LENGTH : (count + k + 1) * PIECE_LENGTH] = innov_ref[:, source]


def halo_pack(ids, expected, innov):
    rows = expected.shape[0]
    shape = jax.ShapeDtypeStruct((rows, 2 * ids.shape[1] * PIECE_LENGTH), jnp.float32)
    return pl.pallas_call(
        halo_kernel,
        out_shape=(shape, shape),
        in_specs=[
            pl.BlockSpec(memory_space=pltpu.SMEM),
            pl.BlockSpec(memory_space=pltpu.VMEM),
            pl.BlockSpec(memory_space=pltpu.VMEM),
        ],
        out_specs=(pl.BlockSpec(memory_space=pltpu.VMEM),) * 2,
        name="halo_pack",
    )(ids, expected, innov)


def window_kernel(half, lists_ref, own_ref, before_ref, after_ref, out_ref):
    rows, width = own_ref.shape
    own_count = width // PIECE_LENGTH
    side = before_ref.shape[1] // (2 * PIECE_LENGTH)
    patches, per = lists_ref.shape

    @pl.loop(0, patches)
    def _(p):
        base = pl.multiple_of(p * rows, rows)
        for k in range(per):
            entry = lists_ref[p, k]
            target = (pl.ds(base, rows), slice(k * PIECE_LENGTH, (k + 1) * PIECE_LENGTH))

            @pl.when(entry < own_count)
            def _():
                out_ref[target] = own_ref[:, pieces(entry)]

            @pl.when((entry >= own_count) & (entry < own_count + side))
            def _():
                out_ref[target] = before_ref[:, pieces(entry - own_count + half * side)]

            @pl.when(entry >= own_count + side)
            def _():
                out_ref[target] = after_ref[:, pieces(entry - own_count - side + half * side)]


def window_pack(half, lists, own, before, after):
    rows = own.shape[0]
    patches, per = lists.shape
    return pl.pallas_call(
        functools.partial(window_kernel, half),
        out_shape=jax.ShapeDtypeStruct((patches * rows, per * PIECE_LENGTH), jnp.float32),
        in_specs=[pl.BlockSpec(memory_space=pltpu.SMEM)]
        + [pl.BlockSpec(memory_space=pltpu.VMEM)] * 3,
        out_specs=pl.BlockSpec(memory_space=pltpu.VMEM),
        name="window_pack",
    )(lists, own, before, after)


def to_owners(rows_by_owner):
    return lax.all_to_all(rows_by_owner, "member", split_axis=0, concat_axis=0, tiled=True)


def masked_gain(states, perturbed, cover_rows):
    realization_records, row_count = states.shape
    centred = states - jnp.mean(states, axis=0, keepdims=True)
    gain = lax.dot_general(
        centred,
        perturbed,
        (((0,), (0,)), ((), ())),
        precision=high,
        preferred_element_type=jnp.float32,
    ) / (realization_records - 1.0)
    cover = jnp.repeat(jnp.repeat(cover_rows, PIECE_LENGTH, axis=1), PIECE_LENGTH, axis=0)
    return gain * cover


def increment(weights, gain):
    return lax.dot_general(
        weights,
        gain,
        (((0,), (1,)), ((), ())),
        precision=high,
        preferred_element_type=jnp.float32,
    )


def body(
    background_realizations,
    realization_expected_data,
    departure_values,
    instrument_dispersion,
    window_piece_offsets,
    window_data_pieces,
    neighbor_piece_ids,
    coupling_indicator,
):
    groups = lax.axis_size("member")
    patch = lax.axis_index("member")
    rows, variable_total = background_realizations.shape
    segment_total = variable_total // PIECE_LENGTH
    per_device = segment_total // groups
    spread = (per_device - 1) // 2
    own_width = per_device * PIECE_LENGTH
    edge = spread * PIECE_LENGTH
    obs_count = realization_expected_data.shape[1] // PIECE_LENGTH
    lists = window_data_pieces[0]
    halo_ids = neighbor_piece_ids[0]

    after_send, before_send = halo_pack(halo_ids, realization_expected_data, departure_values)
    var_blocks = instrument_dispersion.reshape(obs_count, PIECE_LENGTH)
    from_before = shifted(after_send, "region", 1)
    from_after = shifted(before_send, "region", -1)
    var_before = shifted(jnp.take(var_blocks, halo_ids[0], axis=0), "region", 1)
    var_after = shifted(jnp.take(var_blocks, halo_ids[1], axis=0), "region", -1)
    var_ext = jnp.concatenate([var_blocks, var_before, var_after], axis=0)

    expected = to_owners(
        window_pack(0, lists, realization_expected_data, from_before, from_after)
    )
    send_innov = window_pack(1, lists, departure_values, from_before, from_after)
    send_states = (
        background_realizations.reshape(rows, groups, own_width)
        .transpose(1, 0, 2)
        .reshape(groups * rows, own_width)
    )
    arrived = to_owners(jnp.concatenate([send_innov, send_states], axis=1))
    innovated = arrived[:, :LOCAL]
    states = arrived[:, LOCAL:]
    members = states.shape[0]

    own_list = lax.dynamic_index_in_dim(lists, patch, 0, keepdims=False)
    variance = jnp.take(var_ext, own_list, axis=0).reshape(LOCAL)
    perturbed = expected - jnp.mean(expected, axis=0, keepdims=True)
    cov_obs = jnp.dot(
        perturbed.T, perturbed, precision=highest, preferred_element_type=jnp.float32
    ) / (members - 1.0)
    cov_obs = cov_obs + jnp.diag(variance)
    factor = jnp.linalg.cholesky(cov_obs)
    weights = jax.scipy.linalg.cho_solve((factor, True), innovated.T)

    up = [(i, i + 1) for i in range(groups - 1)]
    down = [(i + 1, i) for i in range(groups - 1)]
    low_states = lax.ppermute(states[:, own_width - edge :], "member", up)
    high_states = lax.ppermute(states[:, :edge], "member", down)
    edge_states = jnp.concatenate([low_states, high_states], axis=1)

    cover_all = coupling_indicator[0].astype(jnp.float32)
    first = patch * per_device
    own_cover = lax.dynamic_slice_in_dim(cover_all, first, per_device, axis=0)
    low_ids = jnp.maximum(first - spread + jnp.arange(spread), 0)
    high_ids = jnp.minimum(first + per_device + jnp.arange(spread), segment_total - 1)
    edge_cover = jnp.take(cover_all, jnp.concatenate([low_ids, high_ids]), axis=0)

    own_gain = masked_gain(states, perturbed, own_cover)
    edge_gain = masked_gain(edge_states, perturbed, edge_cover)
    edge_inc = increment(weights, edge_gain)
    inc_high = lax.ppermute(edge_inc[:, :edge], "member", down)
    inc_low = lax.ppermute(edge_inc[:, edge:], "member", up)
    own_inc = increment(weights, own_gain)
    bounds = lax.dynamic_slice_in_dim(window_piece_offsets[0], patch, 2) - first
    block = jnp.arange(own_width) // PIECE_LENGTH
    from_low = (block < bounds[0])[None, :edge]
    from_high = (block >= bounds[1])[None, own_width - edge :]
    result = states + jnp.concatenate(
        [
            jnp.where(from_low, inc_low, own_inc[:, :edge]),
            own_inc[:, edge : own_width - edge],
            jnp.where(from_high, inc_high, own_inc[:, own_width - edge :]),
        ],
        axis=1,
    )
    returned = to_owners(result)
    return (
        returned.reshape(groups, rows, own_width).transpose(1, 0, 2).reshape(rows, variable_total)
    )


def solution(mesh):
    return jax.shard_map(
        body,
        mesh=mesh,
        in_specs=(
            P("member", "region"),
            P("member", "region"),
            P("member", "region"),
            P("region"),
            P("region", None),
            P("region", None, None),
            P("region", None, None),
            P("region", None, None),
        ),
        out_specs=P("member", "region"),
        check_vma=False,
    )
```

```python
import functools

import jax
import jax.numpy as jnp
from jax import lax
from jax.experimental import pallas as pl
from jax.experimental.pallas import tpu as pltpu
from jax.sharding import PartitionSpec as P

PIECE_LENGTH = 128
OBS_PER = 4
LOCAL = 512


highest = lax.Precision.HIGHEST
high = lax.Precision.HIGH


def shifted(block, axis, distance):
    count = lax.axis_size(axis)
    return lax.ppermute(block, axis, [(i, (i + distance) % count) for i in range(count)])


def pieces(start, count=1):
    return pl.ds(pl.multiple_of(start * PIECE_LENGTH, PIECE_LENGTH), count * PIECE_LENGTH)


def halo_kernel(ids_ref, expected_ref, innov_ref, after_ref, before_ref):
    count = ids_ref.shape[1]
    for side, out_ref in ((0, after_ref), (1, before_ref)):
        for k in range(count):
            source = pieces(ids_ref[side, k])
            out_ref[:, k * PIECE_LENGTH : (k + 1) * PIECE_LENGTH] = expected_ref[:, source]
            out_ref[:, (count + k) * PIECE_LENGTH : (count + k + 1) * PIECE_LENGTH] = innov_ref[:, source]


def halo_pack(ids, expected, innov):
    rows = expected.shape[0]
    shape = jax.ShapeDtypeStruct((rows, 2 * ids.shape[1] * PIECE_LENGTH), jnp.float32)
    return pl.pallas_call(
        halo_kernel,
        out_shape=(shape, shape),
        in_specs=[
            pl.BlockSpec(memory_space=pltpu.SMEM),
            pl.BlockSpec(memory_space=pltpu.VMEM),
            pl.BlockSpec(memory_space=pltpu.VMEM),
        ],
        out_specs=(pl.BlockSpec(memory_space=pltpu.VMEM),) * 2,
        name="halo_pack",
    )(ids, expected, innov)


def window_kernel(half, lists_ref, own_ref, before_ref, after_ref, out_ref):
    rows, width = own_ref.shape
    own_count = width // PIECE_LENGTH
    side = before_ref.shape[1] // (2 * PIECE_LENGTH)
    patches, per = lists_ref.shape

    @pl.loop(0, patches)
    def _(p):
        base = pl.multiple_of(p * rows, rows)
        for k in range(per):
            entry = lists_ref[p, k]
            target = (pl.ds(base, rows), slice(k * PIECE_LENGTH, (k + 1) * PIECE_LENGTH))

            @pl.when(entry < own_count)
            def _():
                out_ref[target] = own_ref[:, pieces(entry)]

            @pl.when((entry >= own_count) & (entry < own_count + side))
            def _():
                out_ref[target] = before_ref[:, pieces(entry - own_count + half * side)]

            @pl.when(entry >= own_count + side)
            def _():
                out_ref[target] = after_ref[:, pieces(entry - own_count - side + half * side)]


def window_pack(half, lists, own, before, after):
    rows = own.shape[0]
    patches, per = lists.shape
    return pl.pallas_call(
        functools.partial(window_kernel, half),
        out_shape=jax.ShapeDtypeStruct((patches * rows, per * PIECE_LENGTH), jnp.float32),
        in_specs=[pl.BlockSpec(memory_space=pltpu.SMEM)]
        + [pl.BlockSpec(memory_space=pltpu.VMEM)] * 3,
        out_specs=pl.BlockSpec(memory_space=pltpu.VMEM),
        name="window_pack",
    )(lists, own, before, after)


def to_owners(rows_by_owner):
    return lax.all_to_all(rows_by_owner, "member", split_axis=0, concat_axis=0, tiled=True)


def snake(index, row):
    return index + (index // row) % 2 * (row - 1 - 2 * (index % row))


def split_kernel(in_ref, first_ref, second_ref):
    half = first_ref.shape[1]
    first_ref[...] = in_ref[:, :half]
    second_ref[...] = in_ref[:, half:]


def state_pack(background, groups, row, half):
    rows, total = background.shape
    width = total // groups
    return pl.pallas_call(
        split_kernel,
        grid=(groups,),
        out_shape=(
            jax.ShapeDtypeStruct((groups * rows, half), jnp.float32),
            jax.ShapeDtypeStruct((groups * rows, width - half), jnp.float32),
        ),
        in_specs=[pl.BlockSpec((rows, width), lambda i: (0, snake(i, row)))],
        out_specs=(
            pl.BlockSpec((rows, half), lambda i: (i, 0)),
            pl.BlockSpec((rows, width - half), lambda i: (i, 0)),
        ),
        name="state_pack",
    )(background)


def join_kernel(edge, centre_ref, sides_ref, out_ref):
    width = out_ref.shape[1]
    out_ref[:, :edge] = sides_ref[:, :edge]
    out_ref[:, edge : width - edge] = centre_ref[...]
    out_ref[:, width - edge :] = sides_ref[:, edge:]


def state_join(centre, sides, groups, row):
    rows = centre.shape[0] // groups
    edge = sides.shape[1] // 2
    width = centre.shape[1] + 2 * edge
    return pl.pallas_call(
        functools.partial(join_kernel, edge),
        grid=(groups,),
        out_shape=jax.ShapeDtypeStruct((rows, groups * width), jnp.float32),
        in_specs=[
            pl.BlockSpec((rows, width - 2 * edge), lambda i: (i, 0)),
            pl.BlockSpec((rows, 2 * edge), lambda i: (i, 0)),
        ],
        out_specs=pl.BlockSpec((rows, width), lambda i: (0, snake(i, row))),
        name="state_join",
    )(centre, sides)


def masked_gain(states, perturbed, cover_rows):
    realization_records, row_count = states.shape
    centred = states - jnp.mean(states, axis=0, keepdims=True)
    gain = lax.dot_general(
        centred,
        perturbed,
        (((0,), (0,)), ((), ())),
        precision=high,
        preferred_element_type=jnp.float32,
    ) / (realization_records - 1.0)
    cover = jnp.repeat(jnp.repeat(cover_rows, PIECE_LENGTH, axis=1), PIECE_LENGTH, axis=0)
    return gain * cover


def times_transposed(left, right, precision=high):
    return lax.dot_general(
        left,
        right,
        (((1,), (1,)), ((), ())),
        precision=precision,
        preferred_element_type=jnp.float32,
    )


def factor_block(block):
    lower = jnp.linalg.cholesky(block)
    return lax.linalg.triangular_solve(
        lower, jnp.eye(PIECE_LENGTH, dtype=jnp.float32), left_side=True, lower=True
    )


def factor_step(trailing):
    inverse = factor_block(trailing[:PIECE_LENGTH, :PIECE_LENGTH])
    panel = times_transposed(trailing[PIECE_LENGTH:, :PIECE_LENGTH], inverse, highest)
    rest = trailing[PIECE_LENGTH:, PIECE_LENGTH:] - times_transposed(panel, panel, highest)
    return inverse, panel, rest


def solve_rows(inverses, panels, innovated):
    count = len(inverses)
    rest = innovated
    forward = []
    for k in range(count):
        part = times_transposed(rest[:, :PIECE_LENGTH], inverses[k], highest)
        forward.append(part)
        if k + 1 < count:
            rest = rest[:, PIECE_LENGTH:] - times_transposed(part, panels[k], highest)
    done = None
    for k in reversed(range(count)):
        part = forward[k]
        if done is not None:
            part = part - jnp.dot(
                done, panels[k], precision=highest, preferred_element_type=jnp.float32
            )
        part = jnp.dot(
            part, inverses[k], precision=highest, preferred_element_type=jnp.float32
        )
        done = part if done is None else jnp.concatenate([part, done], axis=1)
    return done


def body(
    row,
    background_realizations,
    realization_expected_data,
    departure_values,
    instrument_dispersion,
    window_piece_offsets,
    window_data_pieces,
    neighbor_piece_ids,
    coupling_indicator,
):
    groups = lax.axis_size("member")
    patch = snake(lax.axis_index("member"), row)
    rows, variable_total = background_realizations.shape
    segment_total = variable_total // PIECE_LENGTH
    per_device = segment_total // groups
    spread = (per_device - 1) // 2
    own_width = per_device * PIECE_LENGTH
    half = per_device // 2 * PIECE_LENGTH
    edge = spread * PIECE_LENGTH
    obs_count = realization_expected_data.shape[1] // PIECE_LENGTH
    lists = window_data_pieces[0]
    sorted_lists = jnp.stack([lists[snake(i, row)] for i in range(groups)])
    halo_ids = neighbor_piece_ids[0]
    up = [(snake(p, row), snake(p + 1, row)) for p in range(groups - 1)]
    down = [(after, before) for before, after in up]

    send_first, send_second = state_pack(background_realizations, groups, row, half)
    first_states = to_owners(send_first)

    after_send, before_send = halo_pack(halo_ids, realization_expected_data, departure_values)
    var_blocks = instrument_dispersion.reshape(obs_count, PIECE_LENGTH)
    from_before = shifted(after_send, "region", 1)
    from_after = shifted(before_send, "region", -1)
    var_before = shifted(jnp.take(var_blocks, halo_ids[0], axis=0), "region", 1)
    var_after = shifted(jnp.take(var_blocks, halo_ids[1], axis=0), "region", -1)
    var_ext = jnp.concatenate([var_blocks, var_before, var_after], axis=0)
    own_list = lax.dynamic_index_in_dim(lists, patch, 0, keepdims=False)
    variance = jnp.take(var_ext, own_list, axis=0).reshape(LOCAL)

    send_expected = window_pack(
        0, sorted_lists, realization_expected_data, from_before, from_after
    )
    send_innov = window_pack(1, sorted_lists, departure_values, from_before, from_after)
    first_states, send_expected, send_innov, variance = lax.optimization_barrier(
        (first_states, send_expected, send_innov, variance)
    )
    expected = to_owners(send_expected)
    expected, send_second, first_states = lax.optimization_barrier(
        (expected, send_second, first_states)
    )
    second_states = to_owners(send_second)
    high_states = lax.ppermute(first_states[:, :edge], "member", down)
    members = first_states.shape[0]

    perturbed = expected - jnp.mean(expected, axis=0, keepdims=True)
    cov_obs = jnp.dot(
        perturbed.T, perturbed, precision=highest, preferred_element_type=jnp.float32
    ) / (members - 1.0)
    trailing = cov_obs + jnp.diag(variance)
    inverses, panels = [], []
    for k in range(OBS_PER):
        if k == OBS_PER // 2:
            trailing, second_states, send_innov = lax.optimization_barrier(
                (trailing, second_states, send_innov)
            )
            innovated = to_owners(send_innov)
            low_states = lax.ppermute(
                second_states[:, own_width - half - edge :], "member", up
            )
        if k + 1 < OBS_PER:
            inverse, panel, trailing = factor_step(trailing)
            panels.append(panel)
        else:
            inverse = factor_block(trailing)
        inverses.append(inverse)
    inverses[-1], innovated = lax.optimization_barrier((inverses[-1], innovated))
    weights = solve_rows(inverses, panels, innovated)

    cover_all = coupling_indicator[0].astype(jnp.float32)
    first = patch * per_device
    cover_pad = jnp.pad(cover_all, ((spread, spread), (0, 0)))
    covers = lax.dynamic_slice_in_dim(cover_pad, first, per_device + 2 * spread, axis=0)
    split = half // PIECE_LENGTH
    low_gain = masked_gain(low_states, perturbed, covers[:spread])
    high_gain = masked_gain(high_states, perturbed, covers[per_device + spread :])
    first_gain = masked_gain(first_states, perturbed, covers[spread : spread + split])
    second_gain = masked_gain(
        second_states, perturbed, covers[spread + split : spread + per_device]
    )
    inc_high = lax.ppermute(times_transposed(weights, low_gain), "member", down)
    inc_low = lax.ppermute(times_transposed(weights, high_gain), "member", up)
    first_inc = times_transposed(weights, first_gain)
    second_inc = times_transposed(weights, second_gain)
    bounds = lax.dynamic_slice_in_dim(window_piece_offsets[0], patch, 2) - first
    block = jnp.arange(own_width) // PIECE_LENGTH
    from_low = (block < bounds[0])[None, :edge]
    from_high = (block >= bounds[1])[None, own_width - edge :]
    tail = own_width - half - edge
    centre = jnp.concatenate(
        [
            first_states[:, edge:] + first_inc[:, edge:],
            second_states[:, :tail] + second_inc[:, :tail],
        ],
        axis=1,
    )
    centre_back = to_owners(centre)
    sides = jnp.concatenate(
        [
            first_states[:, :edge] + jnp.where(from_low, inc_low, first_inc[:, :edge]),
            second_states[:, tail:] + jnp.where(from_high, inc_high, second_inc[:, tail:]),
        ],
        axis=1,
    )
    sides_back = to_owners(sides)
    return state_join(centre_back, sides_back, groups, row)


def row_length(mesh):
    devices = mesh.devices[:, 0].tolist()
    count = len(devices)
    spots = [getattr(d, "coords", None) for d in devices]
    if any(spot is None for spot in spots):
        return count
    row = 1
    while row < count and spots[row][2] == spots[0][2]:
        row += 1
    return row if count % row == 0 else count


def solution(mesh):
    return jax.shard_map(
        functools.partial(body, row_length(mesh)),
        mesh=mesh,
        in_specs=(
            P("member", "region"),
            P("member", "region"),
            P("member", "region"),
            P("region"),
            P("region", None),
            P("region", None, None),
            P("region", None, None),
            P("region", None, None),
        ),
        out_specs=P("member", "region"),
        check_vma=False,
    )
```

```python
import functools

import jax
import jax.numpy as jnp
from jax import lax
from jax.experimental import pallas as pl
from jax.experimental.pallas import tpu as pltpu
from jax.sharding import PartitionSpec as P

PIECE_LENGTH = 128
OBS_PER = 4
LOCAL = 512


highest = lax.Precision.HIGHEST
high = lax.Precision.HIGH


def shifted(block, axis, distance):
    count = lax.axis_size(axis)
    return lax.ppermute(block, axis, [(i, (i + distance) % count) for i in range(count)])


def pieces(start, count=1):
    return pl.ds(pl.multiple_of(start * PIECE_LENGTH, PIECE_LENGTH), count * PIECE_LENGTH)


def halo_kernel(ids_ref, expected_ref, innov_ref, after_ref, before_ref):
    count = ids_ref.shape[1]
    for side, out_ref in ((0, after_ref), (1, before_ref)):
        for k in range(count):
            source = pieces(ids_ref[side, k])
            out_ref[:, k * PIECE_LENGTH : (k + 1) * PIECE_LENGTH] = expected_ref[:, source]
            out_ref[:, (count + k) * PIECE_LENGTH : (count + k + 1) * PIECE_LENGTH] = innov_ref[:, source]


def halo_pack(ids, expected, innov):
    rows = expected.shape[0]
    shape = jax.ShapeDtypeStruct((rows, 2 * ids.shape[1] * PIECE_LENGTH), jnp.float32)
    return pl.pallas_call(
        halo_kernel,
        out_shape=(shape, shape),
        in_specs=[
            pl.BlockSpec(memory_space=pltpu.SMEM),
            pl.BlockSpec(memory_space=pltpu.VMEM),
            pl.BlockSpec(memory_space=pltpu.VMEM),
        ],
        out_specs=(pl.BlockSpec(memory_space=pltpu.VMEM),) * 2,
        name="halo_pack",
    )(ids, expected, innov)


def window_kernel(half, lists_ref, own_ref, before_ref, after_ref, out_ref):
    rows, width = own_ref.shape
    own_count = width // PIECE_LENGTH
    side = before_ref.shape[1] // (2 * PIECE_LENGTH)
    patches, per = lists_ref.shape

    @pl.loop(0, patches)
    def _(p):
        base = pl.multiple_of(p * rows, rows)
        for k in range(per):
            entry = lists_ref[p, k]
            target = (pl.ds(base, rows), slice(k * PIECE_LENGTH, (k + 1) * PIECE_LENGTH))

            @pl.when(entry < own_count)
            def _():
                out_ref[target] = own_ref[:, pieces(entry)]

            @pl.when((entry >= own_count) & (entry < own_count + side))
            def _():
                out_ref[target] = before_ref[:, pieces(entry - own_count + half * side)]

            @pl.when(entry >= own_count + side)
            def _():
                out_ref[target] = after_ref[:, pieces(entry - own_count - side + half * side)]


def window_pack(half, lists, own, before, after):
    rows = own.shape[0]
    patches, per = lists.shape
    return pl.pallas_call(
        functools.partial(window_kernel, half),
        out_shape=jax.ShapeDtypeStruct((patches * rows, per * PIECE_LENGTH), jnp.float32),
        in_specs=[pl.BlockSpec(memory_space=pltpu.SMEM)]
        + [pl.BlockSpec(memory_space=pltpu.VMEM)] * 3,
        out_specs=pl.BlockSpec(memory_space=pltpu.VMEM),
        name="window_pack",
    )(lists, own, before, after)


def to_owners(rows_by_owner):
    return lax.all_to_all(rows_by_owner, "member", split_axis=0, concat_axis=0, tiled=True)


def snake(index, row):
    return index + (index // row) % 2 * (row - 1 - 2 * (index % row))


def split_kernel(in_ref, first_ref, second_ref):
    half = first_ref.shape[1]
    first_ref[...] = in_ref[:, :half]
    second_ref[...] = in_ref[:, half:]


def state_pack(background, groups, row, half):
    rows, total = background.shape
    width = total // groups
    return pl.pallas_call(
        split_kernel,
        grid=(groups,),
        out_shape=(
            jax.ShapeDtypeStruct((groups * rows, half), jnp.float32),
            jax.ShapeDtypeStruct((groups * rows, width - half), jnp.float32),
        ),
        in_specs=[pl.BlockSpec((rows, width), lambda i: (0, snake(i, row)))],
        out_specs=(
            pl.BlockSpec((rows, half), lambda i: (i, 0)),
            pl.BlockSpec((rows, width - half), lambda i: (i, 0)),
        ),
        name="state_pack",
    )(background)


def join_kernel(edge, centre_ref, sides_ref, out_ref):
    width = out_ref.shape[1]
    out_ref[:, :edge] = sides_ref[:, :edge]
    out_ref[:, edge : width - edge] = centre_ref[...]
    out_ref[:, width - edge :] = sides_ref[:, edge:]


def state_join(centre, sides, groups, row):
    rows = centre.shape[0] // groups
    edge = sides.shape[1] // 2
    width = centre.shape[1] + 2 * edge
    return pl.pallas_call(
        functools.partial(join_kernel, edge),
        grid=(groups,),
        out_shape=jax.ShapeDtypeStruct((rows, groups * width), jnp.float32),
        in_specs=[
            pl.BlockSpec((rows, width - 2 * edge), lambda i: (i, 0)),
            pl.BlockSpec((rows, 2 * edge), lambda i: (i, 0)),
        ],
        out_specs=pl.BlockSpec((rows, width), lambda i: (0, snake(i, row))),
        name="state_join",
    )(centre, sides)


def masked_gain(states, perturbed, cover_rows):
    realization_records, row_count = states.shape
    centred = states - jnp.mean(states, axis=0, keepdims=True)
    gain = lax.dot_general(
        centred,
        perturbed,
        (((0,), (0,)), ((), ())),
        precision=high,
        preferred_element_type=jnp.float32,
    ) / (realization_records - 1.0)
    cover = jnp.repeat(jnp.repeat(cover_rows, PIECE_LENGTH, axis=1), PIECE_LENGTH, axis=0)
    return gain * cover


def times_transposed(left, right, precision=high):
    return lax.dot_general(
        left,
        right,
        (((1,), (1,)), ((), ())),
        precision=precision,
        preferred_element_type=jnp.float32,
    )


def factor_kernel(block_ref, inverse_ref, work_ref):
    size = block_ref.shape[0]
    wide = 2 * size
    eye = lax.broadcasted_iota(jnp.int32, (size, size), 0) == lax.broadcasted_iota(
        jnp.int32, (size, size), 1
    )
    work_ref[:, :size] = block_ref[...]
    work_ref[:, size:] = eye.astype(jnp.float32)
    step_rows = 8
    row_ids = lax.broadcasted_iota(jnp.int32, (step_rows, wide), 0)
    for start in range(0, size, step_rows):
        rows = work_ref[start : start + step_rows, :]
        for j in range(step_rows):
            column = rows[:, start + j : start + j + 1]
            scale = 1.0 / jnp.sqrt(column[j : j + 1, :])
            pivot = rows[j : j + 1, :] * scale
            lowered = rows - (column * scale) * pivot
            rows = jnp.where(row_ids > j, lowered, jnp.where(row_ids == j, pivot, rows))
        inverse_ref[start : start + step_rows, :] = rows[:, size:]
        after = start + step_rows
        if after < size:
            change = lax.dot_general(
                rows[:, :size],
                rows,
                (((0,), (0,)), ((), ())),
                precision=highest,
                preferred_element_type=jnp.float32,
            )
            work_ref[after:, :] = work_ref[after:, :] - change[after:, :]


def factor_block(block):
    size = block.shape[0]
    return pl.pallas_call(
        factor_kernel,
        out_shape=jax.ShapeDtypeStruct((size, size), jnp.float32),
        in_specs=[pl.BlockSpec(memory_space=pltpu.VMEM)],
        out_specs=pl.BlockSpec(memory_space=pltpu.VMEM),
        scratch_shapes=[pltpu.VMEM((size, 2 * size), jnp.float32)],
        name="factor_block",
    )(block)


def factor_step(trailing):
    inverse = factor_block(trailing[:PIECE_LENGTH, :PIECE_LENGTH])
    panel = times_transposed(trailing[PIECE_LENGTH:, :PIECE_LENGTH], inverse, highest)
    rest = trailing[PIECE_LENGTH:, PIECE_LENGTH:] - times_transposed(panel, panel, highest)
    return inverse, panel, rest


def solve_rows(inverses, panels, innovated):
    count = len(inverses)
    rest = innovated
    forward = []
    for k in range(count):
        part = times_transposed(rest[:, :PIECE_LENGTH], inverses[k], highest)
        forward.append(part)
        if k + 1 < count:
            rest = rest[:, PIECE_LENGTH:] - times_transposed(part, panels[k], highest)
    done = None
    for k in reversed(range(count)):
        part = forward[k]
        if done is not None:
            part = part - jnp.dot(
                done, panels[k], precision=highest, preferred_element_type=jnp.float32
            )
        part = jnp.dot(
            part, inverses[k], precision=highest, preferred_element_type=jnp.float32
        )
        done = part if done is None else jnp.concatenate([part, done], axis=1)
    return done


def body(
    row,
    background_realizations,
    realization_expected_data,
    departure_values,
    instrument_dispersion,
    window_piece_offsets,
    window_data_pieces,
    neighbor_piece_ids,
    coupling_indicator,
):
    groups = lax.axis_size("member")
    patch = snake(lax.axis_index("member"), row)
    rows, variable_total = background_realizations.shape
    segment_total = variable_total // PIECE_LENGTH
    per_device = segment_total // groups
    spread = (per_device - 1) // 2
    own_width = per_device * PIECE_LENGTH
    half = per_device // 2 * PIECE_LENGTH
    edge = spread * PIECE_LENGTH
    obs_count = realization_expected_data.shape[1] // PIECE_LENGTH
    lists = window_data_pieces[0]
    sorted_lists = jnp.stack([lists[snake(i, row)] for i in range(groups)])
    halo_ids = neighbor_piece_ids[0]
    up = [(snake(p, row), snake(p + 1, row)) for p in range(groups - 1)]
    down = [(after, before) for before, after in up]

    send_first, send_second = state_pack(background_realizations, groups, row, half)
    first_states = to_owners(send_first)

    after_send, before_send = halo_pack(halo_ids, realization_expected_data, departure_values)
    var_blocks = instrument_dispersion.reshape(obs_count, PIECE_LENGTH)
    from_before = shifted(after_send, "region", 1)
    from_after = shifted(before_send, "region", -1)
    var_before = shifted(jnp.take(var_blocks, halo_ids[0], axis=0), "region", 1)
    var_after = shifted(jnp.take(var_blocks, halo_ids[1], axis=0), "region", -1)
    var_ext = jnp.concatenate([var_blocks, var_before, var_after], axis=0)
    own_list = lax.dynamic_index_in_dim(lists, patch, 0, keepdims=False)
    variance = jnp.take(var_ext, own_list, axis=0).reshape(LOCAL)

    send_expected = window_pack(
        0, sorted_lists, realization_expected_data, from_before, from_after
    )
    send_innov = window_pack(1, sorted_lists, departure_values, from_before, from_after)
    first_states, send_expected, send_innov, variance = lax.optimization_barrier(
        (first_states, send_expected, send_innov, variance)
    )
    expected = to_owners(send_expected)
    expected, send_second, first_states = lax.optimization_barrier(
        (expected, send_second, first_states)
    )
    second_states = to_owners(send_second)
    high_states = lax.ppermute(first_states[:, :edge], "member", down)
    members = first_states.shape[0]

    perturbed = expected - jnp.mean(expected, axis=0, keepdims=True)
    cov_obs = jnp.dot(
        perturbed.T, perturbed, precision=highest, preferred_element_type=jnp.float32
    ) / (members - 1.0)
    trailing = cov_obs + jnp.diag(variance)
    inverses, panels = [], []
    for k in range(OBS_PER):
        if k == OBS_PER // 2:
            trailing, second_states, send_innov = lax.optimization_barrier(
                (trailing, second_states, send_innov)
            )
            innovated = to_owners(send_innov)
            low_states = lax.ppermute(
                second_states[:, own_width - half - edge :], "member", up
            )
        if k + 1 < OBS_PER:
            inverse, panel, trailing = factor_step(trailing)
            panels.append(panel)
        else:
            inverse = factor_block(trailing)
        inverses.append(inverse)
    inverses[-1], innovated = lax.optimization_barrier((inverses[-1], innovated))
    weights = solve_rows(inverses, panels, innovated)

    cover_all = coupling_indicator[0].astype(jnp.float32)
    first = patch * per_device
    cover_pad = jnp.pad(cover_all, ((spread, spread), (0, 0)))
    covers = lax.dynamic_slice_in_dim(cover_pad, first, per_device + 2 * spread, axis=0)
    split = half // PIECE_LENGTH
    low_gain = masked_gain(low_states, perturbed, covers[:spread])
    high_gain = masked_gain(high_states, perturbed, covers[per_device + spread :])
    first_gain = masked_gain(first_states, perturbed, covers[spread : spread + split])
    second_gain = masked_gain(
        second_states, perturbed, covers[spread + split : spread + per_device]
    )
    inc_high = lax.ppermute(times_transposed(weights, low_gain), "member", down)
    inc_low = lax.ppermute(times_transposed(weights, high_gain), "member", up)
    first_inc = times_transposed(weights, first_gain)
    second_inc = times_transposed(weights, second_gain)
    bounds = lax.dynamic_slice_in_dim(window_piece_offsets[0], patch, 2) - first
    block = jnp.arange(own_width) // PIECE_LENGTH
    from_low = (block < bounds[0])[None, :edge]
    from_high = (block >= bounds[1])[None, own_width - edge :]
    tail = own_width - half - edge
    centre = jnp.concatenate(
        [
            first_states[:, edge:] + first_inc[:, edge:],
            second_states[:, :tail] + second_inc[:, :tail],
        ],
        axis=1,
    )
    centre_back = to_owners(centre)
    sides = jnp.concatenate(
        [
            first_states[:, :edge] + jnp.where(from_low, inc_low, first_inc[:, :edge]),
            second_states[:, tail:] + jnp.where(from_high, inc_high, second_inc[:, tail:]),
        ],
        axis=1,
    )
    sides_back = to_owners(sides)
    return state_join(centre_back, sides_back, groups, row)


def row_length(mesh):
    devices = mesh.devices[:, 0].tolist()
    count = len(devices)
    spots = [getattr(d, "coords", None) for d in devices]
    if any(spot is None for spot in spots):
        return count
    row = 1
    while row < count and spots[row][2] == spots[0][2]:
        row += 1
    return row if count % row == 0 else count


def solution(mesh):
    return jax.shard_map(
        functools.partial(body, row_length(mesh)),
        mesh=mesh,
        in_specs=(
            P("member", "region"),
            P("member", "region"),
            P("member", "region"),
            P("region"),
            P("region", None),
            P("region", None, None),
            P("region", None, None),
            P("region", None, None),
        ),
        out_specs=P("member", "region"),
        check_vma=False,
    )
```

```python
import functools

import jax
import jax.numpy as jnp
from jax import lax
from jax.experimental import pallas as pl
from jax.experimental.pallas import tpu as pltpu
from jax.sharding import PartitionSpec as P

PIECE_LENGTH = 128
OBS_PER = 4
LOCAL = 512


highest = lax.Precision.HIGHEST
high = lax.Precision.HIGH


def shifted(block, axis, distance):
    count = lax.axis_size(axis)
    return lax.ppermute(block, axis, [(i, (i + distance) % count) for i in range(count)])


def pieces(start, count=1):
    return pl.ds(pl.multiple_of(start * PIECE_LENGTH, PIECE_LENGTH), count * PIECE_LENGTH)


def halo_kernel(ids_ref, expected_ref, innov_ref, after_ref, before_ref):
    count = ids_ref.shape[1]
    for side, out_ref in ((0, after_ref), (1, before_ref)):
        for k in range(count):
            source = pieces(ids_ref[side, k])
            out_ref[:, k * PIECE_LENGTH : (k + 1) * PIECE_LENGTH] = expected_ref[:, source]
            out_ref[:, (count + k) * PIECE_LENGTH : (count + k + 1) * PIECE_LENGTH] = innov_ref[:, source]


def halo_pack(ids, expected, innov):
    rows = expected.shape[0]
    shape = jax.ShapeDtypeStruct((rows, 2 * ids.shape[1] * PIECE_LENGTH), jnp.float32)
    return pl.pallas_call(
        halo_kernel,
        out_shape=(shape, shape),
        in_specs=[
            pl.BlockSpec(memory_space=pltpu.SMEM),
            pl.BlockSpec(memory_space=pltpu.VMEM),
            pl.BlockSpec(memory_space=pltpu.VMEM),
        ],
        out_specs=(pl.BlockSpec(memory_space=pltpu.VMEM),) * 2,
        name="halo_pack",
    )(ids, expected, innov)


def window_kernel(half, lists_ref, own_ref, before_ref, after_ref, out_ref):
    rows, width = own_ref.shape
    own_count = width // PIECE_LENGTH
    side = before_ref.shape[1] // (2 * PIECE_LENGTH)
    patches, per = lists_ref.shape

    @pl.loop(0, patches)
    def _(p):
        base = pl.multiple_of(p * rows, rows)
        for k in range(per):
            entry = lists_ref[p, k]
            target = (pl.ds(base, rows), slice(k * PIECE_LENGTH, (k + 1) * PIECE_LENGTH))

            @pl.when(entry < own_count)
            def _():
                out_ref[target] = own_ref[:, pieces(entry)]

            @pl.when((entry >= own_count) & (entry < own_count + side))
            def _():
                out_ref[target] = before_ref[:, pieces(entry - own_count + half * side)]

            @pl.when(entry >= own_count + side)
            def _():
                out_ref[target] = after_ref[:, pieces(entry - own_count - side + half * side)]


def window_pack(half, lists, own, before, after):
    rows = own.shape[0]
    patches, per = lists.shape
    return pl.pallas_call(
        functools.partial(window_kernel, half),
        out_shape=jax.ShapeDtypeStruct((patches * rows, per * PIECE_LENGTH), jnp.float32),
        in_specs=[pl.BlockSpec(memory_space=pltpu.SMEM)]
        + [pl.BlockSpec(memory_space=pltpu.VMEM)] * 3,
        out_specs=pl.BlockSpec(memory_space=pltpu.VMEM),
        name="window_pack",
    )(lists, own, before, after)


def to_owners(rows_by_owner):
    return lax.all_to_all(rows_by_owner, "member", split_axis=0, concat_axis=0, tiled=True)


def snake(index, row):
    return index + (index // row) % 2 * (row - 1 - 2 * (index % row))


def split_kernel(in_ref, first_ref, second_ref):
    half = first_ref.shape[1]
    first_ref[...] = in_ref[:, :half]
    second_ref[...] = in_ref[:, half:]


def state_pack(background, groups, row, half):
    rows, total = background.shape
    width = total // groups
    return pl.pallas_call(
        split_kernel,
        grid=(groups,),
        out_shape=(
            jax.ShapeDtypeStruct((groups * rows, half), jnp.float32),
            jax.ShapeDtypeStruct((groups * rows, width - half), jnp.float32),
        ),
        in_specs=[pl.BlockSpec((rows, width), lambda i: (0, snake(i, row)))],
        out_specs=(
            pl.BlockSpec((rows, half), lambda i: (i, 0)),
            pl.BlockSpec((rows, width - half), lambda i: (i, 0)),
        ),
        name="state_pack",
    )(background)


def join_kernel(in_ref, out_ref):
    out_ref[...] = in_ref[...]


def state_join(returned, groups, row):
    rows = returned.shape[0] // groups
    width = returned.shape[1]
    return pl.pallas_call(
        join_kernel,
        grid=(groups,),
        out_shape=jax.ShapeDtypeStruct((rows, groups * width), jnp.float32),
        in_specs=[pl.BlockSpec((rows, width), lambda i: (i, 0))],
        out_specs=pl.BlockSpec((rows, width), lambda i: (0, snake(i, row))),
        name="state_join",
    )(returned)


def masked_gain(states, perturbed, cover_rows):
    realization_records, row_count = states.shape
    centred = states - jnp.mean(states, axis=0, keepdims=True)
    gain = lax.dot_general(
        centred,
        perturbed,
        (((0,), (0,)), ((), ())),
        precision=high,
        preferred_element_type=jnp.float32,
    ) / (realization_records - 1.0)
    cover = jnp.repeat(jnp.repeat(cover_rows, PIECE_LENGTH, axis=1), PIECE_LENGTH, axis=0)
    return gain * cover


def times_transposed(left, right, precision=high):
    return lax.dot_general(
        left,
        right,
        (((1,), (1,)), ((), ())),
        precision=precision,
        preferred_element_type=jnp.float32,
    )


def factor_kernel(block_ref, inverse_ref, work_ref):
    size = block_ref.shape[0]
    wide = 2 * size
    eye = lax.broadcasted_iota(jnp.int32, (size, size), 0) == lax.broadcasted_iota(
        jnp.int32, (size, size), 1
    )
    work_ref[:, :size] = block_ref[...]
    work_ref[:, size:] = eye.astype(jnp.float32)
    step_rows = 8
    row_ids = lax.broadcasted_iota(jnp.int32, (step_rows, wide), 0)
    for start in range(0, size, step_rows):
        rows = work_ref[start : start + step_rows, :]
        for j in range(step_rows):
            column = rows[:, start + j : start + j + 1]
            scale = lax.rsqrt(column[j : j + 1, :])
            pivot = rows[j : j + 1, :] * scale
            lowered = rows - (column * scale) * pivot
            rows = jnp.where(row_ids > j, lowered, jnp.where(row_ids == j, pivot, rows))
        inverse_ref[start : start + step_rows, :] = rows[:, size:]
        after = start + step_rows
        if after < size:
            change = lax.dot_general(
                rows[:, :size],
                rows,
                (((0,), (0,)), ((), ())),
                precision=highest,
                preferred_element_type=jnp.float32,
            )
            work_ref[after:, :] = work_ref[after:, :] - change[after:, :]


def factor_block(block):
    size = block.shape[0]
    return pl.pallas_call(
        factor_kernel,
        out_shape=jax.ShapeDtypeStruct((size, size), jnp.float32),
        in_specs=[pl.BlockSpec(memory_space=pltpu.VMEM)],
        out_specs=pl.BlockSpec(memory_space=pltpu.VMEM),
        scratch_shapes=[pltpu.VMEM((size, 2 * size), jnp.float32)],
        name="factor_block",
    )(block)


def factor_step(trailing):
    inverse = factor_block(trailing[:PIECE_LENGTH, :PIECE_LENGTH])
    panel = times_transposed(trailing[PIECE_LENGTH:, :PIECE_LENGTH], inverse, highest)
    rest = trailing[PIECE_LENGTH:, PIECE_LENGTH:] - times_transposed(panel, panel, highest)
    return inverse, panel, rest


def solve_rows(inverses, panels, innovated):
    count = len(inverses)
    rest = innovated
    forward = []
    for k in range(count):
        part = times_transposed(rest[:, :PIECE_LENGTH], inverses[k], highest)
        forward.append(part)
        if k + 1 < count:
            rest = rest[:, PIECE_LENGTH:] - times_transposed(part, panels[k], highest)
    done = None
    for k in reversed(range(count)):
        part = forward[k]
        if done is not None:
            part = part - jnp.dot(
                done, panels[k], precision=highest, preferred_element_type=jnp.float32
            )
        part = jnp.dot(
            part, inverses[k], precision=highest, preferred_element_type=jnp.float32
        )
        done = part if done is None else jnp.concatenate([part, done], axis=1)
    return done


def body(
    row,
    background_realizations,
    realization_expected_data,
    departure_values,
    instrument_dispersion,
    window_piece_offsets,
    window_data_pieces,
    neighbor_piece_ids,
    coupling_indicator,
):
    groups = lax.axis_size("member")
    patch = snake(lax.axis_index("member"), row)
    rows, variable_total = background_realizations.shape
    segment_total = variable_total // PIECE_LENGTH
    per_device = segment_total // groups
    spread = (per_device - 1) // 2
    own_width = per_device * PIECE_LENGTH
    half = per_device // 2 * PIECE_LENGTH
    edge = spread * PIECE_LENGTH
    obs_count = realization_expected_data.shape[1] // PIECE_LENGTH
    lists = window_data_pieces[0]
    sorted_lists = jnp.stack([lists[snake(i, row)] for i in range(groups)])
    halo_ids = neighbor_piece_ids[0]
    up = [(snake(p, row), snake(p + 1, row)) for p in range(groups - 1)]
    down = [(after, before) for before, after in up]

    send_first, send_second = state_pack(background_realizations, groups, row, half)
    first_states = to_owners(send_first)

    after_send, before_send = halo_pack(halo_ids, realization_expected_data, departure_values)
    var_blocks = instrument_dispersion.reshape(obs_count, PIECE_LENGTH)
    from_before = shifted(after_send, "region", 1)
    from_after = shifted(before_send, "region", -1)
    var_before = shifted(jnp.take(var_blocks, halo_ids[0], axis=0), "region", 1)
    var_after = shifted(jnp.take(var_blocks, halo_ids[1], axis=0), "region", -1)
    var_ext = jnp.concatenate([var_blocks, var_before, var_after], axis=0)
    own_list = lax.dynamic_index_in_dim(lists, patch, 0, keepdims=False)
    variance = jnp.take(var_ext, own_list, axis=0).reshape(LOCAL)

    send_expected = window_pack(
        0, sorted_lists, realization_expected_data, from_before, from_after
    )
    send_innov = window_pack(1, sorted_lists, departure_values, from_before, from_after)
    first_states, send_expected, send_innov, variance = lax.optimization_barrier(
        (first_states, send_expected, send_innov, variance)
    )
    expected = to_owners(send_expected)
    expected, send_second, first_states = lax.optimization_barrier(
        (expected, send_second, first_states)
    )
    second_states = to_owners(send_second)
    high_states = lax.ppermute(first_states[:, :edge], "member", down)
    members = first_states.shape[0]

    perturbed = expected - jnp.mean(expected, axis=0, keepdims=True)
    cov_obs = jnp.dot(
        perturbed.T, perturbed, precision=highest, preferred_element_type=jnp.float32
    ) / (members - 1.0)
    trailing = cov_obs + jnp.diag(variance)
    inverses, panels = [], []
    for k in range(OBS_PER):
        if k == OBS_PER // 2:
            trailing, second_states, send_innov = lax.optimization_barrier(
                (trailing, second_states, send_innov)
            )
            innovated = to_owners(send_innov)
            low_states = lax.ppermute(
                second_states[:, own_width - half - edge :], "member", up
            )
        if k + 1 < OBS_PER:
            inverse, panel, trailing = factor_step(trailing)
            panels.append(panel)
        else:
            inverse = factor_block(trailing)
        inverses.append(inverse)
    inverses[-1], innovated = lax.optimization_barrier((inverses[-1], innovated))
    weights = solve_rows(inverses, panels, innovated)

    cover_all = coupling_indicator[0].astype(jnp.float32)
    first = patch * per_device
    cover_pad = jnp.pad(cover_all, ((spread, spread), (0, 0)))
    covers = lax.dynamic_slice_in_dim(cover_pad, first, per_device + 2 * spread, axis=0)
    split = half // PIECE_LENGTH
    low_gain = masked_gain(low_states, perturbed, covers[:spread])
    high_gain = masked_gain(high_states, perturbed, covers[per_device + spread :])
    first_gain = masked_gain(first_states, perturbed, covers[spread : spread + split])
    second_gain = masked_gain(
        second_states, perturbed, covers[spread + split : spread + per_device]
    )
    inc_high = lax.ppermute(times_transposed(weights, low_gain), "member", down)
    inc_low = lax.ppermute(times_transposed(weights, high_gain), "member", up)
    first_inc = times_transposed(weights, first_gain)
    second_inc = times_transposed(weights, second_gain)
    bounds = lax.dynamic_slice_in_dim(window_piece_offsets[0], patch, 2) - first
    block = jnp.arange(own_width) // PIECE_LENGTH
    from_low = (block < bounds[0])[None, :edge]
    from_high = (block >= bounds[1])[None, own_width - edge :]
    tail = own_width - half - edge
    result = jnp.concatenate(
        [
            first_states[:, :edge] + jnp.where(from_low, inc_low, first_inc[:, :edge]),
            first_states[:, edge:] + first_inc[:, edge:],
            second_states[:, :tail] + second_inc[:, :tail],
            second_states[:, tail:] + jnp.where(from_high, inc_high, second_inc[:, tail:]),
        ],
        axis=1,
    )
    return state_join(to_owners(result), groups, row)


def row_length(mesh):
    devices = mesh.devices[:, 0].tolist()
    count = len(devices)
    spots = [getattr(d, "coords", None) for d in devices]
    if any(spot is None for spot in spots):
        return count
    row = 1
    while row < count and spots[row][2] == spots[0][2]:
        row += 1
    return row if count % row == 0 else count


def solution(mesh):
    return jax.shard_map(
        functools.partial(body, row_length(mesh)),
        mesh=mesh,
        in_specs=(
            P("member", "region"),
            P("member", "region"),
            P("member", "region"),
            P("region"),
            P("region", None),
            P("region", None, None),
            P("region", None, None),
            P("region", None, None),
        ),
        out_specs=P("member", "region"),
        check_vma=False,
    )
```
